32 devices in a mesh: gx: 8 (over y, x, core), gy: 4 (over z).
Axes of the slice: x: 2, y: 2, z: 4, core: 2. Of those that a mesh axis runs over, the one named last changes fastest.
Arguments:
- features: bfloat16 [8, 4, 512, 128], P('gx', 'gy'), may hold values from -6 to 6
- cotangent: bfloat16 [8, 4, 512, 128], P('gx', 'gy'), may hold values from -6 to 6
- weight_one: bfloat16 [27, 128, 128], replicated, may hold values from -0.125 to 0.125
- weight_two: bfloat16 [27, 128, 128], replicated, may hold values from -0.125 to 0.125
- block_count: int32 [8, 4], P('gx', 'gy'), may hold values from 4 to 8, as said below
- send_list: int32 [8, 4, 8, 4], P('gx', 'gy'), may hold values from 0 to 7, as said below
- rulebook: int32 [8, 4, 27, 512], P('gx', 'gy'), may hold values from 0 to 2560, as said below
Outputs:
- output: bfloat16 [8, 4, 512, 128], P('gx', 'gy')
- grad_features: bfloat16 [8, 4, 512, 128], P('gx', 'gy')
- grad_one: float32 [27, 128, 128], P(None, 'gx')
- grad_two: float32 [27, 128, 128], P(None, 'gx')
The draws below stay inside these ranges and needn't reach their ends.
Inputs may be any that keep to these rules, and one draw needn't show every extreme that they name: The active blocks of a device are its first block_count blocks; some device has 8. send_list[a, b, e] lists the 4 blocks that device (a, b) sends toward the device at direction d_e; every entry is an active block of the sender; entries may repeat. rulebook[a, b, k, i] is a row of device (a, b)'s extended table; 2560 is the zero row and means no neighbour at that offset. Rows of inactive blocks hold 2560 at every offset; for an active row, offset 13 is the row itself; every other entry below 2560 is an active row of the device or a row of the slot of a neighbouring device that exists.
All inputs are finite; a program needn't handle non-finite values.
Results may differ from the reference program's by a relative error of at most 0.0055.
Values may be sent and summed in bfloat16 or wider, within the bound.
A program may use at most 128 MiB of HBM per device.

```python
import jax
import jax.numpy as jnp
import numpy as np
from jax import lax

C = 128
BLK = 64
NBLK = 8
SEND = 4
EXT = 2560
DEVS = 32
N_GX = 8
N_GY = 4


STEPS_X = np.array([-1, -1, -1, 0, 0, 1, 1, 1], dtype=np.int32)


STEPS_Y = np.array([-1, 0, 1, -1, 1, -1, 0, 1], dtype=np.int32)


def block_layout(key):
    device_total = N_GX * N_GY
    counts = jax.random.randint(jax.random.fold_in(key, 11), (device_total,), NBLK // 2, NBLK + 1)
    fullest = jax.random.randint(jax.random.fold_in(key, 12), (), 0, device_total)
    counts = counts.at[fullest].set(NBLK)
    return (counts.reshape(N_GX, N_GY).astype(jnp.int32), fullest)


def draw_block_count(key, part):
    counts, fullest = block_layout(key)
    return counts


def draw_send_list(key, part):
    counts, fullest = block_layout(key)
    raw_bits = jax.random.randint(jax.random.fold_in(key, 13), (N_GX, N_GY, 8, SEND), 0, 1 << 20)
    listed = raw_bits % counts[:, :, None, None]
    flat_list = listed.reshape(N_GX * N_GY, 8, SEND)
    flat_list = flat_list.at[fullest, 0, 0].set(NBLK - 1)
    flat_list = flat_list.at[fullest, 1, 0].set(0)
    return flat_list.reshape(N_GX, N_GY, 8, SEND).astype(jnp.int32)


def draw_rulebook(key, part):
    counts, fullest = block_layout(key)
    row_total = NBLK * BLK
    table_end = row_total + 8 * SEND * BLK
    shape_all = (N_GX, N_GY, 27, row_total)
    raw_bits = jax.random.randint(jax.random.fold_in(key, 14), shape_all, 0, 1 << 24)
    direction = jax.random.randint(jax.random.fold_in(key, 15), shape_all, 0, 8)
    slot_row = jax.random.randint(jax.random.fold_in(key, 16), shape_all, 0, SEND * BLK)
    place_x = jax.lax.broadcasted_iota(jnp.int32, shape_all, 0)
    place_y = jax.lax.broadcasted_iota(jnp.int32, shape_all, 1)
    offsets = jax.lax.broadcasted_iota(jnp.int32, shape_all, 2)
    row_ids = jax.lax.broadcasted_iota(jnp.int32, shape_all, 3)
    kinds = raw_bits % 8
    picked = raw_bits // 8
    live_rows = counts[:, :, None, None] * BLK
    local_row = picked % live_rows
    other_x = place_x + jnp.asarray(STEPS_X)[direction]
    other_y = place_y + jnp.asarray(STEPS_Y)[direction]
    exists = (other_x >= 0) & (other_x < N_GX) & (other_y >= 0) & (other_y < N_GY)
    halo_row = row_total + direction * (SEND * BLK) + slot_row
    chosen = jnp.where(kinds < 4, table_end, jnp.where((kinds >= 6) & exists, halo_row, local_row))
    chosen = jnp.where(offsets == 13, row_ids, chosen)
    active = row_ids // BLK < counts[:, :, None, None]
    return jnp.where(active, chosen, table_end).astype(jnp.int32)


def strengthened(values, key, source, target, blocks, factor):
    def block_of(dim):
        return (jnp.arange(values.shape[dim]) // (values.shape[dim] // blocks)).reshape((-1,) + (1,) * (values.ndim - 1 - dim))

    near = jax.random.permutation(key, blocks)[block_of(target)]
    other_side = (block_of(target) + blocks // 2) % blocks
    return jnp.where((block_of(source) == near) | (block_of(source) == other_side), factor * values, values)


def block_scale(own_key, extent, pieces, low, top_value):
    level = 1.0
    for axis_at, blocks in pieces:
        draws = jax.random.uniform(jax.random.fold_in(jax.random.fold_in(own_key, 6), axis_at), (blocks,), jnp.float32, low / len(pieces), top_value / len(pieces))
        level = level * jnp.repeat(jnp.exp(draws), extent[axis_at] // blocks).reshape((-1,) + (1,) * (len(extent) - 1 - axis_at))
    return level


def gaussian(rng, dims, spread, reach, split=(), kind=jnp.bfloat16):
    entries = spread * jax.random.normal(rng, dims, jnp.float32)
    if split:
        entries = entries * block_scale(rng, dims, split, -0.22, 0.18)
    return jnp.clip(entries, -reach, reach).astype(kind)


def noise_with(rng, extent, width, most, shards, heavy, kind=jnp.bfloat16):
    values = width * jax.random.normal(rng, extent, jnp.float32)
    if shards:
        values = values * block_scale(rng, extent, shards, -0.22, 0.18)
    return jnp.clip(strengthened(values, jax.random.fold_in(rng, 3), *heavy), -most, most).astype(kind)


def setup_inputs(seed: int = 0) -> dict:
    key_of = jax.random.split(jax.random.key(seed), 8)
    features = noise_with(key_of[0], (N_GX, N_GY, NBLK * BLK, C), 1.0, 6.0, ((0, 8), (1, 4)), (0, 3, 8, 2.0))
    cotangent = gaussian(key_of[1], (N_GX, N_GY, NBLK * BLK, C), 1.0, 6.0, ((0, 8), (1, 4)))
    weight_one = gaussian(key_of[2], (27, C, C), (14 * C) ** -0.5, 0.125)
    weight_two = gaussian(key_of[3], (27, C, C), (14 * C) ** -0.5, 0.125)
    block_count = draw_block_count(jax.random.fold_in(key_of[7], 71), 0)
    send_list = draw_send_list(jax.random.fold_in(key_of[7], 71), 0)
    rulebook = draw_rulebook(jax.random.fold_in(key_of[7], 71), 0)
    return dict(features=features, cotangent=cotangent, weight_one=weight_one, weight_two=weight_two, block_count=block_count, send_list=send_list, rulebook=rulebook)


DIRECTIONS = ((-1, -1), (-1, 0), (-1, 1), (0, -1), (0, 1), (1, -1), (1, 0), (1, 1))

def neighbour(source, step_x, step_y):
    padding = [(1, 1), (1, 1)] + [(0, 0)] * (source.ndim - 2)
    padded = jnp.pad(source, padding)
    return padded[1 + step_x:1 + step_x + N_GX, 1 + step_y:1 + step_y + N_GY]

def take_rows(lookup, chosen):
    return jax.vmap(jax.vmap(lambda table_rows, picked: table_rows[picked]))(lookup, chosen)

def extend_field(field, send_list):
    block_rows = field.reshape(N_GX, N_GY, NBLK, BLK, C)
    outgoing = jax.vmap(jax.vmap(lambda blocks, listed: blocks[listed]))(block_rows, send_list)
    halos = [neighbour(outgoing[:, :, 7 - index_j], step_x, step_y) for index_j, (step_x, step_y) in enumerate(DIRECTIONS)]
    halo_rows = jnp.stack(halos, 2).reshape(N_GX, N_GY, 8 * SEND * BLK, C)
    zero_row = jnp.zeros((N_GX, N_GY, 1, C), field.dtype)
    return jnp.concatenate((field, halo_rows, zero_row), 2)

def conv_forward(extended, rulebook, weight):
    rule_sets = jnp.moveaxis(rulebook, 2, 0)

    def add_offset(totals, item):
        indices, matrix = item
        gathered = take_rows(extended, indices)
        return (totals + jnp.dot(gathered, matrix, preferred_element_type=jnp.float32), None)
    start = jnp.zeros((N_GX, N_GY, NBLK * BLK, C), jnp.float32)
    totals, ignored = lax.scan(add_offset, start, (rule_sets, weight))
    return totals

def conv_transpose(grads, rulebook, weight, send_list):
    rule_sets = jnp.moveaxis(rulebook, 2, 0)

    def add_offset(totals, item):
        indices, matrix = item
        terms = jnp.dot(grads, matrix.T, preferred_element_type=jnp.float32)
        totals = jax.vmap(jax.vmap(lambda table_rows, picked, values: table_rows.at[picked].add(values)))(totals, indices, terms)
        return (totals, None)
    start = jnp.zeros((N_GX, N_GY, EXT + 1, C), jnp.float32)
    totals, ignored = lax.scan(add_offset, start, (rule_sets, weight))
    row_total = NBLK * BLK
    local_blocks = totals[:, :, :row_total].reshape(N_GX, N_GY, NBLK, BLK, C)
    halo_part = totals[:, :, row_total:EXT].astype(jnp.bfloat16)
    halo_part = lax.optimization_barrier(halo_part).astype(jnp.float32)
    halo_part = halo_part.reshape(N_GX, N_GY, 8, SEND, BLK, C)
    for index_j, (step_x, step_y) in enumerate(DIRECTIONS):
        incoming = neighbour(halo_part[:, :, index_j], -step_x, -step_y)
        targets = send_list[:, :, 7 - index_j]
        local_blocks = jax.vmap(jax.vmap(lambda blocks, listed, values: blocks.at[listed].add(values)))(local_blocks, targets, incoming)
    return local_blocks.reshape(N_GX, N_GY, row_total, C)

def weight_grad(extended, rulebook, grads):
    rule_sets = jnp.moveaxis(rulebook, 2, 0)
    flat_grads = grads.reshape(-1, C)

    def one_offset(carried, indices):
        gathered = take_rows(extended, indices).reshape(-1, C)
        return (carried, jnp.dot(gathered.T, flat_grads, preferred_element_type=jnp.float32))
    ignored, stacked = lax.scan(one_offset, jnp.zeros((), jnp.float32), rule_sets)
    return stacked

def reference(features, cotangent, weight_one, weight_two, block_count, send_list, rulebook):
    positions = jnp.arange(NBLK * BLK).astype(jnp.int32) // BLK
    live = (positions[None, None, :] < block_count[:, :, None])[..., None]
    live_float = live.astype(jnp.float32)
    live_half = live.astype(jnp.bfloat16)
    masked = features * live_half
    ext_input = extend_field(masked, send_list)
    first_pre = conv_forward(ext_input, rulebook, weight_one) * live_float
    hidden = jax.nn.silu(first_pre).astype(jnp.bfloat16)
    ext_hidden = extend_field(hidden, send_list)
    output = (conv_forward(ext_hidden, rulebook, weight_two) * live_float).astype(jnp.bfloat16)
    upstream = cotangent * live_half
    grad_hidden = conv_transpose(upstream, rulebook, weight_two, send_list)
    sigmoid_pre = jax.nn.sigmoid(first_pre)
    grad_pre = (grad_hidden * sigmoid_pre * (1.0 + first_pre * (1.0 - sigmoid_pre)) * live_float).astype(jnp.bfloat16)
    grad_features = (conv_transpose(grad_pre, rulebook, weight_one, send_list) * live_float).astype(jnp.bfloat16)
    grad_two = weight_grad(ext_hidden, rulebook, upstream) / DEVS
    grad_one = weight_grad(ext_input, rulebook, grad_pre) / DEVS
    return (output, grad_features, grad_one, grad_two)
```

```python
import jax
import jax.numpy as jnp
from jax import lax
from jax.experimental import pallas as pl
from jax.experimental.pallas import tpu as pltpu
from jax.sharding import PartitionSpec as P

BLK = 64
UNROLL = 3
F32 = jnp.float32
BF16 = jnp.bfloat16

VM = pl.BlockSpec(memory_space=pltpu.VMEM)
SM = pl.BlockSpec(memory_space=pltpu.SMEM)


def shifted(block, axis, distance):
    devices = range(lax.axis_size(axis))
    route = [(i - distance, i) for i in devices if i - distance in devices]
    return lax.ppermute(block, axis, route)


def deliver(left, middle, right):
    from_left = shifted(left, "gx", -1)
    from_right = shifted(right, "gx", 1)
    down = shifted(jnp.stack((from_left[0], middle[0], from_right[0])), "gy", -1)
    up = shifted(jnp.stack((from_left[2], middle[1], from_right[2])), "gy", 1)
    return from_left[1], from_right[1], down, up


def arrived_at(refs, e):
    left, right, down, up = refs
    return (
        lambda: down[0], lambda: left[...], lambda: up[0], lambda: down[1],
        lambda: up[1], lambda: down[2], lambda: right[...], lambda: up[2],
    )[e]()


def live_mask(count, rows):
    ids = lax.broadcasted_iota(jnp.int32, (rows, 1), 0)
    return ids < count * BLK


def put_outgoing(field_ref, send, out_refs, per):
    left, middle, right = out_refs
    for e in range(8):
        target = left.at[e] if e < 3 else middle.at[e - 3] if e < 5 else right.at[e - 5]
        for s in range(per):
            start = pl.multiple_of(send[e, s] * BLK, BLK)
            target[s * BLK : (s + 1) * BLK, :] = field_ref[pl.ds(start, BLK), :]


def column(table, k):
    lanes = lax.broadcasted_iota(jnp.int32, table.shape, 1)
    return jnp.sum(jnp.where(lanes == k, table, 0.0), axis=1, keepdims=True)


def prepare_kernel(count, send, x_ref, g_ref, masked, upstream, left, middle, right):
    rows = x_ref.shape[0]
    live = live_mask(count[0, 0], rows).astype(F32).astype(BF16)
    masked[...] = x_ref[...] * live
    upstream[...] = g_ref[...] * live
    put_outgoing(masked, send, (left, middle, right), send.shape[1])


def scatter_step(k, g, rule, hi, lo, w, acc):
    rows = g.shape[0]
    pieces = acc.shape[1] // g.shape[1]
    terms = lax.dot_general(g, w[k], (((1,), (1,)), ((), ())), preferred_element_type=F32)
    low = column(lo[...], k)
    wide = jnp.concatenate(
        [jnp.where(low == float(p), terms, 0.0).astype(BF16) for p in range(pieces)], axis=1
    )
    picked = rule[pl.ds(k, 1), :] & (rows - 1) if rows & (rows - 1) == 0 else rule[pl.ds(k, 1), :] % rows
    hot = (lax.broadcasted_iota(jnp.int32, (rows, rows), 0) == picked)
    hot = jnp.where(hot, 1.0, 0.0).astype(BF16)
    return jnp.dot(hot, wide, preferred_element_type=F32)


def scatter_loop(g, rule, hi, lo, w, acc, extra=None):
    acc[...] = jnp.zeros_like(acc)

    @pl.loop(0, w.shape[0] // UNROLL)
    def _(step):
        total = None
        for u in range(UNROLL):
            k = step * UNROLL + u
            part = scatter_step(k, g, rule, hi, lo, w, acc)
            total = part if total is None else total + part
            if extra is not None:
                extra(k)
        acc[...] += total


def split_totals(acc, own, left, middle, right, rows, channels):
    own[...] = acc[:, :channels]
    half = rows // 2
    for j in range(8):
        target = left.at[j] if j < 3 else middle.at[j - 3] if j < 5 else right.at[j - 5]
        base = (j % 2) * half
        col = (1 + j // 2) * channels
        target[...] = acc[base : base + half, col : col + channels].astype(BF16)


def first_scatter_kernel(g, rule, hi, lo, w, own, left, middle, right, acc):
    rows, channels = g.shape
    scatter_loop(g[...], rule, hi, lo, w, acc)
    split_totals(acc, own, left, middle, right, rows, channels)


def fill_table(field, refs, table):
    rows, channels = field.shape
    half = rows // 2
    table[:, :channels] = field[...]
    for j in range(8):
        base = (j % 2) * half
        col = (1 + j // 2) * channels
        table[base : base + half, col : col + channels] = arrived_at(refs, 7 - j)


def gather_step(k, hi, lo, table, channels):
    rows = table.shape[0]
    high = column(hi[...], k)
    low = column(lo[...], k)
    ids = lax.broadcasted_iota(jnp.int32, (rows, rows), 1).astype(F32)
    hot = jnp.where(ids == high, 1.0, 0.0).astype(BF16)
    found = jnp.dot(hot, table[...], preferred_element_type=F32)
    picked = jnp.zeros((rows, channels), F32)
    for p in range(table.shape[1] // channels):
        picked = jnp.where(low == float(p), found[:, p * channels : (p + 1) * channels], picked)
    return picked.astype(BF16)


def first_gather_kernel(
    count, send, field, a, b, c, d, hi, lo, w, pre, gathered, hidden, left, middle, right, table
):
    rows, channels = field.shape
    fill_table(field, (a, b, c, d), table)
    pre[...] = jnp.zeros_like(pre)

    @pl.loop(0, w.shape[0] // UNROLL)
    def _(step):
        total = None
        for u in range(UNROLL):
            k = step * UNROLL + u
            picked = gather_step(k, hi, lo, table, channels)
            gathered[k] = picked
            part = jnp.dot(picked, w[k], preferred_element_type=F32)
            total = part if total is None else total + part
        pre[...] += total

    live = live_mask(count[0, 0], rows).astype(F32)
    v = pre[...] * live
    pre[...] = v
    hidden[...] = (v / (1.0 + jnp.exp(-v))).astype(BF16)
    put_outgoing(hidden, send, (left, middle, right), send.shape[1])


def add_returned(send, own, refs, total, per):
    total[...] = own[...]
    for e in range(8):
        block = arrived_at(refs, e).astype(F32)
        for s in range(per):
            start = pl.multiple_of(send[7 - e, s] * BLK, BLK)
            total[pl.ds(start, BLK), :] += block[s * BLK : (s + 1) * BLK, :]


def second_scatter_kernel(
    count, send, grad_own, a, b, c, d, pre, gathered, rule, hi, lo, w,
    own, left, middle, right, partial, acc, total, grad
):
    rows, channels = pre.shape
    add_returned(send, grad_own, (a, b, c, d), total, send.shape[1])
    live = live_mask(count[0, 0], rows).astype(F32)
    v = pre[...]
    s = 1.0 / (1.0 + jnp.exp(-v))
    grad[...] = (total[...] * s * (1.0 + v * (1.0 - s)) * live).astype(BF16)
    g = grad[...]

    def extra(k):
        partial[k] = lax.dot_general(
            gathered[k], g, (((0,), (0,)), ((), ())), preferred_element_type=F32
        )

    scatter_loop(g, rule, hi, lo, w, acc, extra)
    split_totals(acc, own, left, middle, right, rows, channels)


def second_gather_kernel(count, field, a, b, c, d, hi, lo, w, g, out, partial, table, total):
    rows, channels = field.shape
    fill_table(field, (a, b, c, d), table)
    total[...] = jnp.zeros_like(total)
    upstream = g[...]

    @pl.loop(0, w.shape[0] // UNROLL)
    def _(step):
        summed = None
        for u in range(UNROLL):
            k = step * UNROLL + u
            picked = gather_step(k, hi, lo, table, channels)
            partial[k] = lax.dot_general(
                picked, upstream, (((0,), (0,)), ((), ())), preferred_element_type=F32
            )
            part = jnp.dot(picked, w[k], preferred_element_type=F32)
            summed = part if summed is None else summed + part
        total[...] += summed

    live = live_mask(count[0, 0], rows).astype(F32)
    out[...] = (total[...] * live).astype(BF16)


def finish_kernel(count, send, own, a, b, c, d, out, total):
    rows = own.shape[0]
    add_returned(send, own, (a, b, c, d), total, send.shape[1])
    out[...] = (total[...] * live_mask(count[0, 0], rows).astype(F32)).astype(BF16)


def call(kernel, out_shape, in_specs, scratch, flops=0, moved=0):
    return pl.pallas_call(
        kernel,
        out_shape=out_shape,
        in_specs=in_specs,
        out_specs=tuple([VM] * len(out_shape)),
        scratch_shapes=scratch,
        compiler_params=pltpu.CompilerParams(vmem_limit_bytes=48 << 20),
        cost_estimate=pl.CostEstimate(flops=flops, bytes_accessed=moved, transcendentals=0),
    )


def on_device(features, cotangent, weight_one, weight_two, block_count, send_list, rulebook):
    field, cot = features[0, 0], cotangent[0, 0]
    send, rule = send_list[0, 0], rulebook[0, 0]
    rows, channels = field.shape
    kernel = rule.shape[0]
    slot = send.shape[1] * BLK
    shape = jax.ShapeDtypeStruct
    wide = (rows, channels * (1 + 8 * slot // rows))
    columns = jnp.pad(rule.T, ((0, 0), (0, 128 - kernel)))
    hi = (columns % rows).astype(F32)
    lo = (columns // rows).astype(F32)
    flops = 2 * kernel * rows * rows * wide[1]
    moved = 8 << 20
    rows_bf = shape((rows, channels), BF16)
    rows_f = shape((rows, channels), F32)
    groups = (
        shape((3, slot, channels), BF16), shape((2, slot, channels), BF16),
        shape((3, slot, channels), BF16),
    )
    grads = shape((kernel, channels, channels), F32)
    table = pltpu.VMEM(wide, BF16)
    acc = pltpu.VMEM(wide, F32)
    plain = pltpu.VMEM((rows, channels), F32)

    masked, upstream, *out_masked = call(
        prepare_kernel, (rows_bf, rows_bf) + groups, [SM, SM, VM, VM], []
    )(block_count, send, field, cot)
    halo_one = deliver(*out_masked)
    own_two, *back_two = call(
        first_scatter_kernel, (rows_f,) + groups, [VM] * 5, [acc], flops, moved
    )(upstream, rule, hi, lo, weight_two)
    arrived_two = deliver(*back_two)
    pre, gathered, hidden, *out_hidden = call(
        first_gather_kernel,
        (rows_f, shape((kernel, rows, channels), BF16), rows_bf) + groups,
        [SM, SM] + [VM] * 8, [table], flops, moved,
    )(block_count, send, masked, *halo_one, hi, lo, weight_one)
    halo_two = deliver(*out_hidden)
    own_one, *rest = call(
        second_scatter_kernel, (rows_f,) + groups + (grads,),
        [SM, SM] + [VM] * 11,
        [acc, plain, pltpu.VMEM((rows, channels), BF16)], flops, moved,
    )(block_count, send, own_two, *arrived_two, pre, gathered, rule, hi, lo, weight_one)
    *back_one, partial_one = rest
    arrived_one = deliver(*back_one)
    output, partial_two = call(
        second_gather_kernel, (rows_bf, grads), [SM] + [VM] * 9, [table, plain], flops, moved
    )(block_count, hidden, *halo_two, hi, lo, weight_two, upstream)
    (grad_input,) = call(finish_kernel, (rows_bf,), [SM, SM] + [VM] * 5, [plain])(
        block_count, send, own_one, *arrived_one
    )
    device_total = lax.axis_size("gx") * lax.axis_size("gy")
    slab_one = lax.psum_scatter(partial_one, "gx", scatter_dimension=1, tiled=True)
    slab_two = lax.psum_scatter(partial_two, "gx", scatter_dimension=1, tiled=True)
    summed_one, summed_two = lax.psum((slab_one, slab_two), "gy")
    return (
        output[None, None],
        grad_input[None, None],
        summed_one / device_total,
        summed_two / device_total,
    )


def solution(mesh):
    placed = (
        P("gx", "gy", None, None),
        P("gx", "gy", None, None),
        P(),
        P(),
        P("gx", "gy"),
        P("gx", "gy", None, None),
        P("gx", "gy", None, None),
    )
    return jax.shard_map(
        on_device,
        mesh=mesh,
        in_specs=placed,
        out_specs=(
            P("gx", "gy", None, None),
            P("gx", "gy", None, None),
            P(None, "gx", None),
            P(None, "gx", None),
        ),
        check_vma=False,
    )
```

```python
import functools

import jax
import jax.numpy as jnp
from jax import lax
from jax.experimental import pallas as pl
from jax.experimental.pallas import tpu as pltpu
from jax.sharding import PartitionSpec as P

BLK = 64
UNROLL = 3
GROUPS = 3
F32 = jnp.float32
BF16 = jnp.bfloat16
MESH = pl.DeviceIdType.MESH
DIRECTIONS = ((-1, -1), (-1, 0), (-1, 1), (0, -1), (0, 1), (1, -1), (1, 0), (1, 1))

VM = pl.BlockSpec(memory_space=pltpu.VMEM)
SM = pl.BlockSpec(memory_space=pltpu.SMEM)


def column(table, k):
    lanes = lax.broadcasted_iota(jnp.int32, table.shape, 1)
    return jnp.sum(jnp.where(lanes == k, table, 0.0), axis=1, keepdims=True)


def whole_kernel(
    nx, ny,
    count, send, features, cotangent, rule, hi, lo, w1, w2,
    output, grad_input, grad_one, grad_two,
    table1, table2, field, hidden, upstream, grad, pre, gathered, acc, own1, own2, sums,
    outs, backs, rets, gsend, grecv, ysend, yrecv,
    halo_ss, halo_rs, gss, grs, yss, yrs,
):
    a, b = lax.axis_index("gx"), lax.axis_index("gy")
    nblk, blk, channels = field.shape
    rows = nblk * blk
    half = rows // 2
    kernel = w1.shape[0]
    per = send.shape[1]
    slot = per * blk
    chunk = channels // nx
    span = kernel // GROUPS
    pieces = acc.shape[1] // channels

    def exists(e):
        dx, dy = DIRECTIONS[e]
        x, y = a + dx, b + dy
        return (x >= 0) & (x < nx) & (y >= 0) & (y < ny)

    def place(e):
        dx, dy = DIRECTIONS[e]
        return (a + dx, b + dy)

    def gx_peer(off):
        return (lax.rem(a + off, nx), b)

    def gy_peer(off):
        return (a, lax.rem(b + off, ny))

    table1[...] = jnp.zeros_like(table1)
    table2[...] = jnp.zeros_like(table2)
    rets[...] = jnp.zeros_like(rets)

    barrier = pltpu.get_barrier_semaphore()
    for off in range(1, nx):
        pl.semaphore_signal(barrier, inc=1, device_id=gx_peer(off), device_id_type=MESH)
    for off in range(1, ny):
        pl.semaphore_signal(barrier, inc=1, device_id=gy_peer(off), device_id_type=MESH)
    corners = (0, 2, 5, 7)
    for e in corners:
        dx, dy = DIRECTIONS[e]
        corner = (lax.rem(a + dx + nx, nx), lax.rem(b + dy + ny, ny))
        pl.semaphore_signal(barrier, inc=1, device_id=corner, device_id_type=MESH)

    ids = lax.broadcasted_iota(jnp.int32, (rows, 1), 0)
    live = (ids < count[0, 0] * blk).astype(F32)
    masked = (features[...].astype(F32) * live).astype(BF16)
    field[...] = masked.reshape(nblk, blk, channels)
    upstream[...] = (cotangent[...].astype(F32) * live).astype(BF16)
    table1[:, :channels] = masked

    pl.semaphore_wait(barrier, nx - 1 + ny - 1 + len(corners))

    def slot_view(table, j):
        return table.at[pl.ds((j % 2) * half, half), pl.ds((1 + j // 2) * channels, channels)]

    def ext_copy(x, e, table):
        return pltpu.make_async_remote_copy(
            src_ref=outs.at[x, e], dst_ref=slot_view(table, 7 - e),
            send_sem=halo_ss.at[x, e], recv_sem=halo_rs.at[x, 7 - e],
            device_id=place(e), device_id_type=MESH,
        )

    def back_copy(x, j):
        return pltpu.make_async_remote_copy(
            src_ref=backs.at[x, j], dst_ref=rets.at[x, j],
            send_sem=halo_ss.at[2 + x, j], recv_sem=halo_rs.at[2 + x, j],
            device_id=place(j), device_id_type=MESH,
        )

    def send_ext(x, source, table):
        for e in range(8):
            for s in range(per):
                outs[x, e, s * blk : (s + 1) * blk, :] = source[send[e, s]]

            @pl.when(exists(e))
            def _():
                ext_copy(x, e, table).start()

    def wait_ext(x, table):
        for e in range(8):
            @pl.when(exists(7 - e))
            def _():
                ext_copy(x, e, table).wait_recv()

    def send_back(x):
        for j in range(8):
            base = (j % 2) * half
            col = (1 + j // 2) * channels
            backs[x, j] = acc[base : base + half, col : col + channels].astype(BF16)

            @pl.when(exists(j))
            def _():
                back_copy(x, j).start()

    def wait_back(x):
        for j in range(8):
            @pl.when(exists(7 - j))
            def _():
                back_copy(x, j).wait_recv()

    def returned_total(x, own):
        for n in range(nblk):
            total = own[n * blk : (n + 1) * blk, :]
            for e in range(8):
                for s in range(per):
                    share = jnp.where(send[7 - e, s] == n, 1.0, 0.0)
                    total += share * rets[x, e, s * blk : (s + 1) * blk, :].astype(F32)
            own[n * blk : (n + 1) * blk, :] = total

    def scatter(k, g, w):
        terms = lax.dot_general(g, w[k], (((1,), (1,)), ((), ())), preferred_element_type=F32)
        low = column(lo[...], k)
        wide = jnp.concatenate(
            [jnp.where(low == float(p), terms, 0.0).astype(BF16) for p in range(pieces)], axis=1
        )
        picked = rule[pl.ds(k, 1), :]
        hot = lax.broadcasted_iota(jnp.int32, (rows, rows), 0) == lax.rem(picked, rows)
        hot = jnp.where(hot, 1.0, 0.0).astype(BF16)
        return jnp.dot(hot, wide, preferred_element_type=F32)

    def gather(k, table):
        high, low = column(hi[...], k), column(lo[...], k)
        lanes = lax.broadcasted_iota(jnp.int32, (rows, rows), 1).astype(F32)
        hot = jnp.where(lanes == high, 1.0, 0.0).astype(BF16)
        found = jnp.dot(hot, table[...], preferred_element_type=F32)
        picked = jnp.zeros((rows, channels), F32)
        for p in range(pieces):
            picked = jnp.where(low == float(p), found[:, p * channels : (p + 1) * channels], picked)
        return picked.astype(BF16)

    def run(start, stop, body, into):
        @pl.loop(start // UNROLL, stop // UNROLL)
        def _(step):
            total = None
            for u in range(UNROLL):
                part = body(step * UNROLL + u)
                total = part if total is None else total + part
            into[...] += total

    def keep_partial(t, k, rows_in, rows_out):
        part = lax.dot_general(rows_in, rows_out, (((0,), (0,)), ((), ())), preferred_element_type=F32)
        at = k - (t % GROUPS) * span
        for p in range(nx):
            gsend[t, p, at] = part[p * chunk : (p + 1) * chunk, :].astype(BF16)

    def gx_copy(t, off):
        peer = gx_peer(off)
        return pltpu.make_async_remote_copy(
            src_ref=gsend.at[t, peer[0]], dst_ref=grecv.at[t, off],
            send_sem=gss.at[t, off], recv_sem=grs.at[t, off],
            device_id=peer, device_id_type=MESH,
        )

    def gy_copy(t, off):
        return pltpu.make_async_remote_copy(
            src_ref=ysend.at[t], dst_ref=yrecv.at[t, off],
            send_sem=yss.at[t, off], recv_sem=yrs.at[t, off],
            device_id=gy_peer(off), device_id_type=MESH,
        )

    def reduce_gx(t):
        total = gsend[t, a].astype(F32)
        for off in range(1, nx):
            gx_copy(t, off).wait_recv()
            total += grecv[t, off].astype(F32)
        ysend[t] = total.astype(BF16)
        for off in range(1, ny):
            gy_copy(t, off).start()

    def reduce_gy(t):
        for off in range(1, ny):
            gy_copy(t, off).wait_recv()
        total = jnp.zeros(ysend.shape[1:], F32)
        for source in range(ny):
            term = jnp.where(source == b, ysend[t].astype(F32), 0.0)
            for off in range(1, ny):
                here = lax.rem(b - off + ny, ny) == source
                term = jnp.where(here, yrecv[t, off].astype(F32), term)
            total += term
        out = grad_one if t < GROUPS else grad_two
        first = (t % GROUPS) * span
        out[first : first + span] = total * (1.0 / (nx * ny))

    def after_group(t):
        for off in range(1, nx):
            gx_copy(t, off).start()
        if t >= 1:
            reduce_gx(t - 1)
        if t >= 2:
            reduce_gy(t - 2)

    send_ext(0, field, table1)
    acc[...] = jnp.zeros_like(acc)
    run(0, kernel, lambda k: scatter(k, upstream[...], w2), acc)
    send_back(0)
    own2[...] = acc[:, :channels]

    wait_ext(0, table1)
    pre[...] = jnp.zeros_like(pre)

    def first_conv(k):
        picked = gather(k, table1)
        gathered[k] = picked
        return jnp.dot(picked, w1[k], preferred_element_type=F32)

    run(0, kernel, first_conv, pre)
    v = pre[...] * live
    pre[...] = v
    hid = (v / (1.0 + jnp.exp(-v))).astype(BF16)
    hidden[...] = hid.reshape(nblk, blk, channels)
    table2[:, :channels] = hid
    send_ext(1, hidden, table2)

    wait_back(0)
    returned_total(0, own2)
    v = pre[...]
    s = 1.0 / (1.0 + jnp.exp(-v))
    grad[...] = (own2[...] * s * (1.0 + v * (1.0 - s)) * live).astype(BF16)
    acc[...] = jnp.zeros_like(acc)
    for t in range(GROUPS):
        def second_scatter(k, t=t):
            keep_partial(t, k, gathered[k], grad[...])
            return scatter(k, grad[...], w1)

        run(t * span, (t + 1) * span, second_scatter, acc)
        after_group(t)
    send_back(1)
    own1[...] = acc[:, :channels]

    wait_ext(1, table2)
    sums[...] = jnp.zeros_like(sums)
    for t in range(GROUPS, 2 * GROUPS):
        def second_conv(k, t=t):
            picked = gather(k, table2)
            keep_partial(t, k, picked, upstream[...])
            return jnp.dot(picked, w2[k], preferred_element_type=F32)

        run((t - GROUPS) * span, (t + 1 - GROUPS) * span, second_conv, sums)
        after_group(t)
    output[...] = (sums[...] * live).astype(BF16)
    wait_back(1)
    returned_total(1, own1)
    grad_input[...] = (own1[...] * live).astype(BF16)
    last = 2 * GROUPS - 1
    reduce_gx(last)
    reduce_gy(last - 1)
    reduce_gy(last)

    for e in range(8):
        @pl.when(exists(e))
        def _():
            ext_copy(0, e, table1).wait_send()
            ext_copy(1, e, table2).wait_send()
            back_copy(0, e).wait_send()
            back_copy(1, e).wait_send()
    for t in range(2 * GROUPS):
        for off in range(1, nx):
            gx_copy(t, off).wait_send()
        for off in range(1, ny):
            gy_copy(t, off).wait_send()


def on_device(features, cotangent, weight_one, weight_two, block_count, send_list, rulebook):
    field, cot = features[0, 0], cotangent[0, 0]
    send, rule = send_list[0, 0], rulebook[0, 0]
    rows, channels = field.shape
    kernel = rule.shape[0]
    slot = send.shape[1] * BLK
    nx, ny = lax.axis_size("gx"), lax.axis_size("gy")
    chunk = channels // nx
    span = kernel // GROUPS
    wide = (rows, channels * (1 + 8 * slot // rows))
    columns = jnp.pad(rule.T, ((0, 0), (0, 128 - kernel)))
    hi = (columns % rows).astype(F32)
    lo = (columns // rows).astype(F32)
    shape = jax.ShapeDtypeStruct
    grads = shape((kernel, chunk, channels), F32)
    plain_f = pltpu.VMEM((rows, channels), F32)
    plain_b = pltpu.VMEM((rows, channels), BF16)
    blocks = pltpu.VMEM((rows // BLK, BLK, channels), BF16)
    halos = pltpu.VMEM((2, 8, slot, channels), BF16)
    parts = 2 * GROUPS
    sem = pltpu.SemaphoreType.DMA
    output, grad_input, one, two = pl.pallas_call(
        functools.partial(whole_kernel, nx, ny),
        out_shape=(shape((rows, channels), BF16),) * 2 + (grads, grads),
        in_specs=[SM, SM] + [VM] * 7,
        out_specs=(VM,) * 4,
        scratch_shapes=[
            pltpu.VMEM(wide, BF16), pltpu.VMEM(wide, BF16), blocks, blocks, plain_b, plain_b,
            plain_f, pltpu.VMEM((kernel, rows, channels), BF16), pltpu.VMEM(wide, F32),
            plain_f, plain_f, plain_f, halos, halos, halos,
            pltpu.VMEM((parts, nx, span, chunk, channels), BF16),
            pltpu.VMEM((parts, nx, span, chunk, channels), BF16),
            pltpu.VMEM((parts, span, chunk, channels), BF16),
            pltpu.VMEM((parts, ny, span, chunk, channels), BF16),
            sem((4, 8)), sem((4, 8)), sem((parts, nx)), sem((parts, nx)),
            sem((parts, ny)), sem((parts, ny)),
        ],
        compiler_params=pltpu.CompilerParams(
            vmem_limit_bytes=56 << 20, collective_id=0, has_side_effects=True
        ),
    )(block_count, send, field, cot, rule, hi, lo, weight_one, weight_two)
    return output[None, None], grad_input[None, None], one, two


def solution(mesh):
    placed = (
        P("gx", "gy", None, None),
        P("gx", "gy", None, None),
        P(),
        P(),
        P("gx", "gy"),
        P("gx", "gy", None, None),
        P("gx", "gy", None, None),
    )
    return jax.shard_map(
        on_device,
        mesh=mesh,
        in_specs=placed,
        out_specs=(
            P("gx", "gy", None, None),
            P("gx", "gy", None, None),
            P(None, "gx", None),
            P(None, "gx", None),
        ),
        check_vma=False,
    )
```

```python
import functools

import jax
import jax.numpy as jnp
from jax import lax
from jax.experimental import pallas as pl
from jax.experimental.pallas import tpu as pltpu
from jax.sharding import PartitionSpec as P

BLK = 64
UNROLL = 3
GROUPS = 3
F32 = jnp.float32
BF16 = jnp.bfloat16
MESH = pl.DeviceIdType.MESH
DIRECTIONS = ((-1, -1), (-1, 0), (-1, 1), (0, -1), (0, 1), (1, -1), (1, 0), (1, 1))

VM = pl.BlockSpec(memory_space=pltpu.VMEM)
SM = pl.BlockSpec(memory_space=pltpu.SMEM)


def column(table, k):
    lanes = lax.broadcasted_iota(jnp.int32, table.shape, 1)
    return jnp.sum(jnp.where(lanes == k, table, 0.0), axis=1, keepdims=True)


def whole_kernel(
    nx, ny,
    count, send, features, cotangent, rule, hi, lo, w1, w2,
    output, grad_input, grad_one, grad_two,
    table1, table2, field, hidden, upstream, grad, pre, gathered, acc, own1, own2, sums,
    outs, backs, rets, gsend, grecv, ysend, yrecv,
    halo_ss, halo_rs, gss, grs, yss, yrs,
):
    a, b = lax.axis_index("gx"), lax.axis_index("gy")
    nblk, blk, channels = field.shape
    rows = nblk * blk
    half = rows // 2
    kernel = w1.shape[0]
    per = send.shape[1]
    slot = per * blk
    chunk = channels // nx
    span = kernel // GROUPS
    pieces = acc.shape[1] // channels

    def exists(e):
        dx, dy = DIRECTIONS[e]
        x, y = a + dx, b + dy
        return (x >= 0) & (x < nx) & (y >= 0) & (y < ny)

    def place(e):
        dx, dy = DIRECTIONS[e]
        return (a + dx, b + dy)

    def gx_peer(off):
        return (lax.rem(a + off, nx), b)

    def gy_peer(off):
        return (a, lax.rem(b + off, ny))

    table1[...] = jnp.zeros_like(table1)
    table2[...] = jnp.zeros_like(table2)
    rets[...] = jnp.zeros_like(rets)

    barrier = pltpu.get_barrier_semaphore()
    for off in range(1, nx):
        pl.semaphore_signal(barrier, inc=1, device_id=gx_peer(off), device_id_type=MESH)
    for off in range(1, ny):
        pl.semaphore_signal(barrier, inc=1, device_id=gy_peer(off), device_id_type=MESH)
    corners = (0, 2, 5, 7)
    for e in corners:
        dx, dy = DIRECTIONS[e]
        corner = (lax.rem(a + dx + nx, nx), lax.rem(b + dy + ny, ny))
        pl.semaphore_signal(barrier, inc=1, device_id=corner, device_id_type=MESH)

    ids = lax.broadcasted_iota(jnp.int32, (rows, 1), 0)
    live = (ids < count[0, 0] * blk).astype(F32)
    masked = (features[...].astype(F32) * live).astype(BF16)
    field[...] = masked.reshape(nblk, blk, channels)
    upstream[...] = (cotangent[...].astype(F32) * live).astype(BF16)
    table1[:, :channels] = masked

    pl.semaphore_wait(barrier, nx - 1 + ny - 1 + len(corners))

    def slot_view(table, j):
        return table.at[pl.ds((j % 2) * half, half), pl.ds((1 + j // 2) * channels, channels)]

    def ext_copy(x, e, table):
        return pltpu.make_async_remote_copy(
            src_ref=outs.at[x, e], dst_ref=slot_view(table, 7 - e),
            send_sem=halo_ss.at[x, e], recv_sem=halo_rs.at[x, 7 - e],
            device_id=place(e), device_id_type=MESH,
        )

    def back_copy(x, j):
        return pltpu.make_async_remote_copy(
            src_ref=backs.at[x, j], dst_ref=rets.at[x, j],
            send_sem=halo_ss.at[2 + x, j], recv_sem=halo_rs.at[2 + x, j],
            device_id=place(j), device_id_type=MESH,
        )

    def send_ext(x, source, table):
        for e in range(8):
            for s in range(per):
                outs[x, e, s * blk : (s + 1) * blk, :] = source[send[e, s]]

            @pl.when(exists(e))
            def _():
                ext_copy(x, e, table).start()

    def wait_ext(x, table):
        for e in range(8):
            @pl.when(exists(7 - e))
            def _():
                ext_copy(x, e, table).wait_recv()

    def send_back(x):
        for j in range(8):
            base = (j % 2) * half
            col = (1 + j // 2) * channels
            backs[x, j] = acc[base : base + half, col : col + channels].astype(BF16)

            @pl.when(exists(j))
            def _():
                back_copy(x, j).start()

    def wait_back(x):
        for j in range(8):
            @pl.when(exists(7 - j))
            def _():
                back_copy(x, j).wait_recv()

    def returned_total(x, own):
        for n in range(nblk):
            total = own[n * blk : (n + 1) * blk, :]
            for e in range(8):
                for s in range(per):
                    share = jnp.where(send[7 - e, s] == n, 1.0, 0.0)
                    total += share * rets[x, e, s * blk : (s + 1) * blk, :].astype(F32)
            own[n * blk : (n + 1) * blk, :] = total

    def stacked(w, ks):
        return w[pl.ds(ks[0], UNROLL)].reshape(UNROLL * channels, channels)

    def scatter(ks, g, w):
        terms = lax.dot_general(
            g, stacked(w, ks), (((1,), (1,)), ((), ())), preferred_element_type=F32
        )
        tall, hots = [], []
        for u, k in enumerate(ks):
            low = column(lo[...], k)
            term = terms[:, u * channels : (u + 1) * channels]
            tall.append(jnp.concatenate(
                [jnp.where(low == float(p), term, 0.0).astype(BF16) for p in range(pieces)], axis=1
            ))
            picked = rule[pl.ds(k, 1), :]
            hot = lax.broadcasted_iota(jnp.int32, (rows, rows), 0) == lax.rem(picked, rows)
            hots.append(jnp.where(hot, 1.0, 0.0).astype(BF16))
        return jnp.dot(
            jnp.concatenate(hots, axis=1), jnp.concatenate(tall, axis=0), preferred_element_type=F32
        )

    def gather(k, table):
        high, low = column(hi[...], k), column(lo[...], k)
        lanes = lax.broadcasted_iota(jnp.int32, (rows, rows), 1).astype(F32)
        hot = jnp.where(lanes == high, 1.0, 0.0).astype(BF16)
        found = jnp.dot(hot, table[...], preferred_element_type=F32)
        picked = jnp.zeros((rows, channels), F32)
        for p in range(pieces):
            picked = jnp.where(low == float(p), found[:, p * channels : (p + 1) * channels], picked)
        return picked.astype(BF16)

    def run(start, stop, body, into):
        @pl.loop(start // UNROLL, stop // UNROLL)
        def _(step):
            into[...] += body([step * UNROLL + u for u in range(UNROLL)])

    def keep_partial(t, ks, rows_in, rows_out):
        part = lax.dot_general(rows_in, rows_out, (((0,), (0,)), ((), ())), preferred_element_type=F32)
        for u, k in enumerate(ks):
            at = k - (t % GROUPS) * span
            for p in range(nx):
                first = u * channels + p * chunk
                gsend[t, p, at] = part[first : first + chunk, :].astype(BF16)

    def gx_copy(t, off):
        peer = gx_peer(off)
        return pltpu.make_async_remote_copy(
            src_ref=gsend.at[t, peer[0]], dst_ref=grecv.at[t, off],
            send_sem=gss.at[t, off], recv_sem=grs.at[t, off],
            device_id=peer, device_id_type=MESH,
        )

    def gy_copy(t, off):
        return pltpu.make_async_remote_copy(
            src_ref=ysend.at[t], dst_ref=yrecv.at[t, off],
            send_sem=yss.at[t, off], recv_sem=yrs.at[t, off],
            device_id=gy_peer(off), device_id_type=MESH,
        )

    def reduce_gx(t):
        total = gsend[t, a].astype(F32)
        for off in range(1, nx):
            gx_copy(t, off).wait_recv()
            total += grecv[t, off].astype(F32)
        ysend[t] = total.astype(BF16)
        for off in range(1, ny):
            gy_copy(t, off).start()

    def reduce_gy(t):
        for off in range(1, ny):
            gy_copy(t, off).wait_recv()
        total = jnp.zeros(ysend.shape[1:], F32)
        for source in range(ny):
            term = jnp.where(source == b, ysend[t].astype(F32), 0.0)
            for off in range(1, ny):
                here = lax.rem(b - off + ny, ny) == source
                term = jnp.where(here, yrecv[t, off].astype(F32), term)
            total += term
        out = grad_one if t < GROUPS else grad_two
        first = (t % GROUPS) * span
        out[first : first + span] = total * (1.0 / (nx * ny))

    def after_group(t):
        for off in range(1, nx):
            gx_copy(t, off).start()
        if t >= 1:
            reduce_gx(t - 1)
        if t >= 2:
            reduce_gy(t - 2)

    send_ext(0, field, table1)
    acc[...] = jnp.zeros_like(acc)
    run(0, kernel, lambda ks: scatter(ks, upstream[...], w2), acc)
    send_back(0)
    own2[...] = acc[:, :channels]

    wait_ext(0, table1)
    pre[...] = jnp.zeros_like(pre)

    def first_conv(ks):
        picks = [gather(k, table1) for k in ks]
        for k, picked in zip(ks, picks):
            gathered[k] = picked
        return jnp.dot(
            jnp.concatenate(picks, axis=1), stacked(w1, ks), preferred_element_type=F32
        )

    run(0, kernel, first_conv, pre)
    v = pre[...] * live
    pre[...] = v
    hid = (v / (1.0 + jnp.exp(-v))).astype(BF16)
    hidden[...] = hid.reshape(nblk, blk, channels)
    table2[:, :channels] = hid
    send_ext(1, hidden, table2)

    wait_back(0)
    returned_total(0, own2)
    v = pre[...]
    s = 1.0 / (1.0 + jnp.exp(-v))
    grad[...] = (own2[...] * s * (1.0 + v * (1.0 - s)) * live).astype(BF16)
    acc[...] = jnp.zeros_like(acc)
    for t in range(GROUPS):
        def second_scatter(ks, t=t):
            picks = jnp.concatenate([gathered[k] for k in ks], axis=1)
            keep_partial(t, ks, picks, grad[...])
            return scatter(ks, grad[...], w1)

        run(t * span, (t + 1) * span, second_scatter, acc)
        after_group(t)
    send_back(1)
    own1[...] = acc[:, :channels]

    wait_ext(1, table2)
    sums[...] = jnp.zeros_like(sums)
    for t in range(GROUPS, 2 * GROUPS):
        def second_conv(ks, t=t):
            picks = jnp.concatenate([gather(k, table2) for k in ks], axis=1)
            keep_partial(t, ks, picks, upstream[...])
            return jnp.dot(picks, stacked(w2, ks), preferred_element_type=F32)

        run((t - GROUPS) * span, (t + 1 - GROUPS) * span, second_conv, sums)
        after_group(t)
    output[...] = (sums[...] * live).astype(BF16)
    wait_back(1)
    returned_total(1, own1)
    grad_input[...] = (own1[...] * live).astype(BF16)
    last = 2 * GROUPS - 1
    reduce_gx(last)
    reduce_gy(last - 1)
    reduce_gy(last)

    for e in range(8):
        @pl.when(exists(e))
        def _():
            ext_copy(0, e, table1).wait_send()
            ext_copy(1, e, table2).wait_send()
            back_copy(0, e).wait_send()
            back_copy(1, e).wait_send()
    for t in range(2 * GROUPS):
        for off in range(1, nx):
            gx_copy(t, off).wait_send()
        for off in range(1, ny):
            gy_copy(t, off).wait_send()


def on_device(features, cotangent, weight_one, weight_two, block_count, send_list, rulebook):
    field, cot = features[0, 0], cotangent[0, 0]
    send, rule = send_list[0, 0], rulebook[0, 0]
    rows, channels = field.shape
    kernel = rule.shape[0]
    slot = send.shape[1] * BLK
    nx, ny = lax.axis_size("gx"), lax.axis_size("gy")
    chunk = channels // nx
    span = kernel // GROUPS
    wide = (rows, channels * (1 + 8 * slot // rows))
    columns = jnp.pad(rule.T, ((0, 0), (0, 128 - kernel)))
    hi = (columns % rows).astype(F32)
    lo = (columns // rows).astype(F32)
    shape = jax.ShapeDtypeStruct
    grads = shape((kernel, chunk, channels), F32)
    plain_f = pltpu.VMEM((rows, channels), F32)
    plain_b = pltpu.VMEM((rows, channels), BF16)
    blocks = pltpu.VMEM((rows // BLK, BLK, channels), BF16)
    halos = pltpu.VMEM((2, 8, slot, channels), BF16)
    parts = 2 * GROUPS
    sem = pltpu.SemaphoreType.DMA
    output, grad_input, one, two = pl.pallas_call(
        functools.partial(whole_kernel, nx, ny),
        out_shape=(shape((rows, channels), BF16),) * 2 + (grads, grads),
        in_specs=[SM, SM] + [VM] * 7,
        out_specs=(VM,) * 4,
        scratch_shapes=[
            pltpu.VMEM(wide, BF16), pltpu.VMEM(wide, BF16), blocks, blocks, plain_b, plain_b,
            plain_f, pltpu.VMEM((kernel, rows, channels), BF16), pltpu.VMEM(wide, F32),
            plain_f, plain_f, plain_f, halos, halos, halos,
            pltpu.VMEM((parts, nx, span, chunk, channels), BF16),
            pltpu.VMEM((parts, nx, span, chunk, channels), BF16),
            pltpu.VMEM((parts, span, chunk, channels), BF16),
            pltpu.VMEM((parts, ny, span, chunk, channels), BF16),
            sem((4, 8)), sem((4, 8)), sem((parts, nx)), sem((parts, nx)),
            sem((parts, ny)), sem((parts, ny)),
        ],
        compiler_params=pltpu.CompilerParams(
            vmem_limit_bytes=56 << 20, collective_id=0, has_side_effects=True
        ),
    )(block_count, send, field, cot, rule, hi, lo, weight_one, weight_two)
    return output[None, None], grad_input[None, None], one, two


def solution(mesh):
    placed = (
        P("gx", "gy", None, None),
        P("gx", "gy", None, None),
        P(),
        P(),
        P("gx", "gy"),
        P("gx", "gy", None, None),
        P("gx", "gy", None, None),
    )
    return jax.shard_map(
        on_device,
        mesh=mesh,
        in_specs=placed,
        out_specs=(
            P("gx", "gy", None, None),
            P("gx", "gy", None, None),
            P(None, "gx", None),
            P(None, "gx", None),
        ),
        check_vma=False,
    )
```
